32 devices in a mesh: sub: 16 (over z, y, x), mode: 2 (over core).
Axes of the slice: x: 2, y: 2, z: 4, core: 2. Of those that a mesh axis runs over, the one named last changes fastest.
Arguments:
- coupling: bfloat16 [1024, 64, 128], P('sub'), may hold values from -0.5 to 0.5
- coupling_pairs: int32 [1024, 2], P('sub'), may hold values from 0 to 3, as said below
- modes: bfloat16 [1024, 256, 256], P('sub', None, 'mode'), may hold values from -6 to 6
- mode_weights: bfloat16 [1024, 256], P('sub', 'mode'), may hold values from 0 to 1, as said below
- parent_of: int32 [1024, 1], P('sub'), may hold values from 0 to 15; in each aligned block of 64 rows (0 to 63, 64 to 127, ...) at most 8 rows name the same one
- row_block: int32 [1024], P('sub'), may hold values from 0 to 7
- parent_modes: bfloat16 [16, 512, 256], P('sub'), may hold values from -1 to 1
- parent_eigs: float32 [16, 256], P('sub'), may hold values from 0.02 to 0.5
Outputs:
- strengths: float32 [1024, 256], P('sub', 'mode')
The draws below stay inside these ranges and needn't reach their ends.
Inputs may be any that keep to these rules, and one draw needn't show every extreme that they name: `coupling_pairs`: within each child the 2 block indices are distinct. `parent_of`: the 64 children of one index of sub name any one parent at most 8 times; some parent is named exactly 8 times by some index's children. `mode_weights`: Positive.
All inputs are finite; a program needn't handle non-finite values.
Results may differ from the reference program's by a relative error of at most 0.0015.
Values may be sent and summed in bfloat16 or wider, within the bound.
A program may use at most 128 MiB of HBM per device.

```python
import math
import jax
import jax.numpy as jnp
import numpy as np
from jax import lax

M = 256
MP = 256
BLK = 64
NBC = 4
KB = 2
SB = 8
CH_DEV = 64
CHILDREN = 1024
PARENTS = 16
CAPD = 8
N_SUB = 16


def draw_coupling_pairs(key, part):
    scores = jax.random.randint(jax.random.fold_in(key, 11), (CHILDREN, NBC), 0, 1 << 20)
    scores = scores * NBC + jnp.arange(NBC, dtype=jnp.int32)[None, :]
    order = jnp.argsort(scores, axis=1, stable=True)
    return order[:, :KB].astype(jnp.int32)


def draw_mode_weights(key, part):
    level = jax.random.uniform(jax.random.fold_in(key, 23), (CHILDREN, M), jnp.float32, math.log(0.5), 0.0)
    falloff = jnp.arange(M, dtype=jnp.float32) / (M - 1)
    values = jnp.exp(level) * jnp.exp(-math.log(3.0) * falloff)[None, :]
    return values.astype(jnp.bfloat16)


def draw_parent_modes(key, part):
    base = jax.random.normal(jax.random.fold_in(key, 31), (PARENTS, SB * BLK, MP), jnp.float32)
    left = jax.random.normal(jax.random.fold_in(key, 37), (PARENTS, SB * BLK, 1), jnp.float32)
    right = jax.random.normal(jax.random.fold_in(key, 41), (PARENTS, 1, MP), jnp.float32)
    base = jnp.clip(base, -4.0, 4.0)
    left = jnp.clip(left, -3.0, 3.0)
    right = jnp.clip(right, -3.0, 3.0)
    return ((base + 0.6 * left * right) / 10.0).astype(jnp.bfloat16)


def place_ends(result, own_key, least, largest):
    spot = [jax.random.randint(jax.random.fold_in(own_key, axis), (), 0, length) for axis, length in enumerate(result.shape)]
    widest = result.shape.index(max(result.shape))
    beside = spot[:widest] + [(spot[widest] + 1) % result.shape[widest]] + spot[widest + 1:]
    return result.at[tuple(spot)].set(least).at[tuple(beside)].set(largest)


def block_levels(rng, extent, shards, least, top_value):
    factor_of = 1.0
    for dim, shards_of in shards:
        draws = jax.random.uniform(jax.random.fold_in(jax.random.fold_in(rng, 6), dim), (shards_of,), jnp.float32, least / len(shards), top_value / len(shards))
        factor_of = factor_of * jnp.repeat(jnp.exp(draws), extent[dim] // shards_of).reshape((-1,) + (1,) * (len(extent) - 1 - dim))
    return factor_of


def deal_out(rng, own, number, rows, count, top, bound, skew):
    order = jax.random.permutation(rng, count)
    heavy_load, ordinary = portions_of(count, rows * top, bound, skew, True), portions_of(count, rows * top, bound, skew, False)
    places = jnp.arange(count)

    def named(lengths, rotation):
        used = int((lengths > 0).sum())
        fixed = max(1, used // 4)
        passed = fixed + (places - fixed + rotation * (used - fixed)) % max(1, count - fixed)
        return jnp.zeros((count,), jnp.int32).at[order[jnp.where(places < fixed, places, passed)]].set(jnp.asarray(lengths, jnp.int32))

    lengths = jnp.where(number % 4 == 0, named(heavy_load, number // 4), named(ordinary, number - number // 4 - 1))
    mixed = jax.random.permutation(jax.random.fold_in(own, 3), count)
    donor, taker = mixed[0:count // 2 * 2:2], mixed[1:count // 2 * 2:2]
    margin = jnp.minimum(lengths[donor] - 1, bound - lengths[taker]) // 2
    margin = jnp.where((donor == order[0]) | (taker == order[0]) | (lengths[taker] == 0), 0, jnp.maximum(margin, 0))
    passed = jax.random.randint(jax.random.fold_in(own, 4), (count // 2,), 0, 1 << 20) % (margin + 1)
    lengths = lengths.at[donor].add(-passed).at[taker].add(passed)
    members = jnp.searchsorted(jnp.cumsum(lengths), jnp.arange(rows * top), side="right").astype(jnp.int32)
    listing = members.reshape(top, rows).T
    listing = listing[jax.random.permutation(jax.random.fold_in(own, 1), rows)]
    rotation = jax.random.randint(jax.random.fold_in(own, 2), (rows, 1), 0, top)
    return jnp.take_along_axis(listing, (jnp.arange(top)[None, :] + rotation) % top, axis=1)


def portions_of(amount, total, reach, skew, full):
    portions = [(1 << 20) // math.isqrt(rank ** skew) + 1 for rank in range(1, amount + 1)]
    largest = reach if full else min(reach, max(-(-total // amount), total * portions[0] // sum(portions)))
    least = 1 if total - largest >= amount - 1 else 0
    holding, spare = [largest] + [least] * (amount - 1), total - largest - least * (amount - 1)
    while spare > 0:
        movable = [i for i in range(1, amount) if holding[i] < largest] or [i for i in range(1, amount) if holding[i] < reach]
        pool, remaining = sum([portions[i] for i in movable]), spare
        for i in movable:
            more = min(reach - holding[i], max(1, remaining * portions[i] // pool), spare)
            holding[i] = holding[i] + more
            spare = spare - more
    return np.array(holding)


def normal_values(own_key, extent, scale, most, shards=(), kind=jnp.bfloat16):
    result = scale * jax.random.normal(own_key, extent, jnp.float32)
    if shards:
        result = result * block_levels(own_key, extent, shards, -0.22, 0.18)
    return jnp.clip(result, -most, most).astype(kind)


def setup_inputs(seed: int = 0) -> dict:
    keys = jax.random.split(jax.random.key(seed), 9)
    coupling = normal_values(keys[0], (CHILDREN, BLK, KB * BLK), (KB * BLK) ** -0.5, 0.5, ((0, 16),))
    coupling_pairs = draw_coupling_pairs(jax.random.fold_in(keys[8], 71), 0)
    modes = normal_values(keys[2], (CHILDREN, NBC * BLK, M), 1.0, 6.0, ((0, 16), (2, 2)))
    mode_weights = draw_mode_weights(jax.random.fold_in(keys[8], 71), 0)
    parent_of_keys = jax.random.split(jax.random.fold_in(keys[4], 1), CHILDREN // CH_DEV)
    parent_of_turns = jax.random.permutation(jax.random.fold_in(keys[4], 3), CHILDREN // CH_DEV)
    parent_of = jax.vmap(lambda own, number: deal_out(jax.random.fold_in(keys[4], 2), own, number, CH_DEV, N_SUB, 1, CAPD, 2))(parent_of_keys, parent_of_turns).reshape((CHILDREN, 1))
    row_block = place_ends(jax.random.randint(keys[5], (CHILDREN,), 0, SB), jax.random.fold_in(keys[5], 1), 0, SB - 1).astype(jnp.int32)
    parent_modes = draw_parent_modes(jax.random.fold_in(keys[8], 71), 0)
    parent_eigs = jnp.clip(jnp.exp(math.log(0.5) - 3.218876 * jax.random.uniform(keys[7], (PARENTS, MP), jnp.float32) ** block_levels(keys[7], (PARENTS, MP), ((0, 16),), -0.2, 0.2)), 0.02, 0.5)
    return {"coupling": coupling, "coupling_pairs": coupling_pairs, "modes": modes, "mode_weights": mode_weights, "parent_of": parent_of, "row_block": row_block, "parent_modes": parent_modes, "parent_eigs": parent_eigs}


def reference(coupling, coupling_pairs, modes, mode_weights, parent_of, row_block, parent_modes, parent_eigs):
    parent_blocks = parent_modes.reshape(PARENTS, SB, BLK, MP)

    def projected_of(child):
        picked = modes[child].reshape(NBC, BLK, M)[coupling_pairs[child]].reshape(KB * BLK, M)
        record = jnp.dot(coupling[child].astype(jnp.float32), picked.astype(jnp.float32), preferred_element_type=jnp.float32)
        record = (record * mode_weights[child][None, :].astype(jnp.float32)).astype(jnp.bfloat16)
        parent_rows = parent_blocks[parent_of[child, 0], row_block[child]]
        return jnp.dot(parent_rows.T.astype(jnp.float32), record.astype(jnp.float32), preferred_element_type=jnp.float32).astype(jnp.bfloat16)

    def accumulate(gram_sum, child):
        projected = projected_of(child)
        term = jnp.dot(projected.astype(jnp.float32), projected.T.astype(jnp.float32), preferred_element_type=jnp.float32)
        return (gram_sum.at[parent_of[child, 0]].add(term), None)
    children = jnp.arange(CHILDREN).astype(jnp.int32)
    gram_sum, _ = lax.scan(accumulate, jnp.zeros((PARENTS, MP, MP), jnp.float32), children)
    pencil = gram_sum / (CH_DEV * M) + jax.vmap(jnp.diag)(parent_eigs)
    factor = jnp.linalg.cholesky(pencil)
    identity = jnp.eye(MP, dtype=pencil.dtype)
    inverse = jax.vmap(lambda lower: lax.linalg.triangular_solve(lower, identity, left_side=True, lower=True))(factor).astype(jnp.bfloat16)

    def strength(child):
        projected = projected_of(child)
        rotated = jnp.dot(inverse[parent_of[child, 0]].astype(jnp.float32), projected.astype(jnp.float32), preferred_element_type=jnp.float32)
        return jnp.sum(rotated * rotated, axis=0) / MP
    return lax.map(strength, children)
```

```python
import functools

import jax
import jax.numpy as jnp
from jax import lax
from jax.experimental import pallas as pl
from jax.experimental.pallas import tpu as pltpu
from jax.sharding import PartitionSpec as P

MESH = pl.DeviceIdType.MESH
F32 = jnp.float32
BF16 = jnp.bfloat16
HALVES = 2


def dot(a, b, dims=((1,), (0,)), precision=None):
    return lax.dot_general(a, b, (dims, ((), ())), preferred_element_type=F32, precision=precision)


def exact(a, b, dims=((1,), (0,))):
    return dot(a, b, dims, lax.Precision.HIGHEST)


def split(x, terms):
    parts = []
    for _ in range(terms):
        part = x.astype(BF16)
        parts.append(part)
        x = x - part.astype(F32)
    return parts


def placed(record, right):
    zero = jnp.zeros_like(record)
    return jnp.concatenate(
        [jnp.where(right == 0, record, zero), jnp.where(right == 0, zero, record)], axis=0
    )


def record_kernel(
    children, group, parents, pair_ref, owner_ref, row_ref, coupling_ref, modes_ref, weight_ref, record_ref, gram_ref
):
    step = pl.program_id(0)

    @pl.when(step == 0)
    def _():
        @pl.loop(0, gram_ref.shape[0])
        def _(i):
            gram_ref[i] = jnp.zeros(gram_ref.shape[1:], F32)

    for i in range(group):
        child = step * group + i
        picked = jnp.concatenate(
            [modes_ref[i, pair_ref[child, k]] for k in range(pair_ref.shape[1])], axis=0
        )
        record = dot(coupling_ref[i], picked) * weight_ref[pl.ds(i, 1), :].astype(F32)
        record = record.astype(BF16)
        record_ref[i] = record
        block = row_ref[child]
        slot = ((block // 4) * 2 + (block // 2) % 2) * parents + owner_ref[child, 0]
        gram_ref[slot] += dot(record, placed(record, block % 2), ((1,), (1,)))


def records_and_grams(coupling, pairs, modes, weights, owner, row_block, parents):
    children, block, width = coupling.shape
    columns = modes.shape[2]
    blocks = modes.shape[1] // block
    group = 8
    return pl.pallas_call(
        functools.partial(record_kernel, children, group, parents),
        grid_spec=pltpu.PrefetchScalarGridSpec(
            num_scalar_prefetch=3,
            grid=(children // group,),
            in_specs=[
                pl.BlockSpec((group, block, width), lambda i, *_: (i, 0, 0)),
                pl.BlockSpec((group, blocks, block, columns), lambda i, *_: (i, 0, 0, 0)),
                pl.BlockSpec((group, columns), lambda i, *_: (i, 0)),
            ],
            out_specs=[
                pl.BlockSpec((group, block, columns), lambda i, *_: (i, 0, 0)),
                pl.BlockSpec((4 * parents, block, 2 * block), lambda i, *_: (0, 0, 0)),
            ],
        ),
        out_shape=[
            jax.ShapeDtypeStruct((children, block, columns), BF16),
            jax.ShapeDtypeStruct((4 * parents, block, 2 * block), F32),
        ],
        name="records",
    )(pairs, owner, row_block, coupling, modes.reshape(children, blocks, block, columns), weights)


def invert_block(matrix):
    size = matrix.shape[0]
    rows = 8
    lane = lax.broadcasted_iota(jnp.int32, (rows, size), 1)
    row = lax.broadcasted_iota(jnp.int32, (rows, size), 0)

    def turn(_, tiles):
        tiles = list(tiles)
        for j in range(rows):
            at_lane = lane == j
            pivot_row = jnp.broadcast_to(tiles[0][j : j + 1, :], (rows, size))
            scale = 1.0 / jnp.broadcast_to(tiles[0][j : j + 1, j : j + 1], (rows, size))
            scaled = jnp.where(at_lane, scale, pivot_row * scale)
            for t in range(len(tiles)):
                column = jnp.broadcast_to(tiles[t][:, j : j + 1], (rows, size))
                tiles[t] = jnp.where(at_lane, 0.0, tiles[t]) - column * scaled
            tiles[0] = jnp.where(row == j, scaled, tiles[0])
        tiles = tiles[1:] + tiles[:1]
        return tuple(pltpu.roll(t, size - rows, 1) for t in tiles)

    tiles = tuple(matrix[i * rows : (i + 1) * rows, :] for i in range(size // rows))
    tiles = lax.fori_loop(0, size // rows, turn, tiles)
    return jnp.concatenate(tiles, axis=0)


def exchange_kernel(
    subs, scale, owner_ref, row_ref, gram_ref, record_ref, parent_ref, eig_ref,
    out_ref,
    factor_ref, work,
    sib, recv_a, recv_b, recv_c, tile, tile_sib, spread, send_sem, recv_sem,
):
    zs = subs // 4
    me = lax.axis_index("sub")
    core = lax.axis_index("mode")
    z, y, x = me // 4, (me // 2) % 2, me % 2

    def place(zz, yy, xx):
        return ((zz * 2 + yy) * 2 + xx, core)

    sibling = (me, 1 - core)
    near_x, near_y = place(z, y, 1 - x), place(z, 1 - y, x)
    far = [place((z + d) % zs, y, x) for d in range(1, zs)]

    barrier = pltpu.get_barrier_semaphore()
    for peer in [sibling, near_x, near_y] + far:
        pl.semaphore_signal(barrier, inc=1, device_id=peer, device_id_type=MESH)
    pl.semaphore_wait(barrier, 3 + len(far))

    count = [0]

    def send(src, dst, peer):
        k = count[0]
        count[0] += 1
        copy = pltpu.make_async_remote_copy(
            src_ref=src, dst_ref=dst, send_sem=send_sem.at[k], recv_sem=recv_sem.at[k],
            device_id=peer, device_id_type=MESH,
        )
        copy.start()
        return copy

    copies = [send(gram_ref.at[1 - core, k], sib.at[k], sibling) for k in range(HALVES)]
    first = []
    for k in range(HALVES):
        copies[k].wait()

        @pl.loop(0, zs)
        def _(zz, k=k):
            for yy in range(2):
                for xx in range(2):
                    sib[k, zz, yy, xx] += gram_ref[core, k, zz, yy, xx]

        if k == 0:
            first.append(send(sib.at[0, :, :, 1 - x], recv_a.at[0], near_x))
        else:
            first.append(send(sib.at[1, :, 1 - y], recv_a.at[1], near_y))
    second = []
    for k in range(HALVES):
        first[k].wait()

        @pl.loop(0, zs)
        def _(zz, k=k):
            for i in range(2):
                mine = sib[0, zz, i, x] if k == 0 else sib[1, zz, y, i]
                recv_a[k, zz, i] += mine

        if k == 0:
            second.append(send(recv_a.at[0, :, 1 - y], recv_b.at[0], near_y))
        else:
            second.append(send(recv_a.at[1, :, 1 - x], recv_b.at[1], near_x))
    for k in range(HALVES):
        second[k].wait()

        @pl.loop(0, zs)
        def _(zz, k=k):
            recv_b[k, zz] += recv_a[k, zz, y if k == 0 else x]

    third = []
    for d in range(1, zs):
        there = (z + d) % zs
        third.append(send(recv_b.at[:, there], recv_c.at[d - 1], far[d - 1]))
    total = recv_b[:, z]
    for d in range(1, zs):
        third[d - 1].wait()
        total = total + recv_c[d - 1]
    tile[core] = total
    pair = send(tile.at[core], tile.at[core], sibling)
    pair.wait()

    size = parent_ref.shape[1]
    block = tile.shape[2]
    for h in range(2):
        for k in range(HALVES):
            both = split(tile[h, k], 3)
            for r in range(2):
                b = (h * 2 + k) * 2 + r
                rows = parent_ref[b * block : (b + 1) * block, :]
                part = sum(dot(t[:, r * block : (r + 1) * block], rows) for t in both)
                factor_ref[b * block : (b + 1) * block, :] = part
    total = jnp.zeros((size, size), F32)
    for part in split(factor_ref[...], 3):
        total = total + dot(parent_ref[...], part, ((0,), (0,)))
    diagonal = lax.broadcasted_iota(jnp.int32, (size, size), 0) == lax.broadcasted_iota(
        jnp.int32, (size, size), 1
    )
    work[...] = jnp.where(diagonal, eig_ref[...], 0.0) + total * scale

    half = size // 2
    top = invert_block(work[:half, :half])
    cross = work[:half, half:]
    ratio = exact(top, cross)
    corner = invert_block(work[half:, half:] - exact(cross, ratio, ((0,), (0,))))
    side = exact(ratio, corner)
    work[half:, half:] = corner
    work[:half, half:] = -side
    work[half:, :half] = -side.T
    work[:half, :half] = top + exact(side, ratio, ((1,), (1,)))

    span = 2 * HALVES * block
    mine = parent_ref[pl.ds(pl.multiple_of(core * span, span), span), :]
    turned = sum(dot(mine, part) for part in split(work[...], 3))
    factor_ref[:span, :] = turned
    for k in range(HALVES):
        for r in range(2):
            at = (k * 2 + r) * block
            rows = factor_ref[at : at + block, :]
            base = parent_ref[pl.ds(pl.multiple_of(core * span + at, block), block), :]
            value = sum(dot(part, base, ((1,), (1,))) for part in split(rows, 2))
            for t, part in enumerate(split(value, 2)):
                tile_sib[k, t, :, r * block : (r + 1) * block] = part

    for k in range(HALVES):
        for t in range(2):
            spread[core, k, z, y, x, t] = tile_sib[k, t]
    own = [send(spread.at[core, :, z, y, x], spread.at[core, :, z, y, x], peer) for peer in far]
    for copy in own:
        copy.wait()
    a = spread.at[core, 0, :, y, x]
    b = spread.at[core, 1, :, y, x]
    up = [send(a, a, near_y), send(b, b, near_x)]
    for copy in up:
        copy.wait()
    a = spread.at[core, 0, :, :, x]
    b = spread.at[core, 1, :, y]
    last = [send(a, a, near_x), send(b, b, near_y)]
    across = [
        send(spread.at[core, 0, :, :, x], spread.at[core, 0, :, :, x], sibling),
        send(spread.at[core, 1, :, y], spread.at[core, 1, :, y], sibling),
    ]
    for copy in last:
        copy.wait()
    across.append(send(spread.at[core, 0, :, :, 1 - x], spread.at[core, 0, :, :, 1 - x], sibling))
    across.append(send(spread.at[core, 1, :, 1 - y], spread.at[core, 1, :, 1 - y], sibling))
    for copy in across:
        copy.wait()

    group = 8

    @pl.loop(0, record_ref.shape[0] // group)
    def _(step):
        values = []
        for i in range(group):
            child = step * group + i
            record = record_ref[child]
            parent, row = owner_ref[child, 0], row_ref[child]
            form = spread[row // 4, (row // 2) % 2, parent // 4, (parent // 2) % 2, parent % 2]
            pushed = dot(form.reshape(2 * block, 2 * block), placed(record, row % 2))
            pushed = pushed[:block] + pushed[block:]
            values.append(jnp.sum(record.astype(F32) * pushed, axis=0, keepdims=True))
        out_ref[pl.ds(pl.multiple_of(step * group, group), group), :] = (
            jnp.concatenate(values, axis=0) / size
        )


def strengths(owner, row_block, grams, records, parent, eigs, subs, scale):
    children, block, columns = records.shape
    rows, size = parent.shape
    zs = subs // 4
    tile = (block, 2 * block)
    copies = 16 + 2 * (zs - 1)
    vmem = pl.BlockSpec(memory_space=pltpu.VMEM)
    smem = pl.BlockSpec(memory_space=pltpu.SMEM)
    return pl.pallas_call(
        functools.partial(exchange_kernel, subs, scale),
        in_specs=[smem, smem, vmem, vmem, vmem, vmem],
        out_specs=vmem,
        out_shape=jax.ShapeDtypeStruct((children, columns), F32),
        scratch_shapes=[
            pltpu.VMEM((rows, size), F32),
            pltpu.VMEM((size, size), F32),
            pltpu.VMEM((HALVES, zs, 2, 2) + tile, F32),
            pltpu.VMEM((HALVES, zs, 2) + tile, F32),
            pltpu.VMEM((HALVES, zs) + tile, F32),
            pltpu.VMEM((max(1, zs - 1), HALVES) + tile, F32),
            pltpu.VMEM((2, HALVES) + tile, F32),
            pltpu.VMEM((HALVES, 2) + tile, BF16),
            pltpu.VMEM((2, HALVES, zs, 2, 2, 2) + tile, BF16),
            pltpu.SemaphoreType.DMA((copies,)),
            pltpu.SemaphoreType.DMA((copies,)),
        ],
        compiler_params=pltpu.CompilerParams(
            collective_id=0, has_side_effects=True, vmem_limit_bytes=60 << 20
        ),
        name="exchange",
    )(owner, row_block, grams.reshape((2, HALVES, zs, 2, 2) + tile), records, parent, eigs)


def per_device(
    coupling, coupling_pairs, modes, mode_weights, parent_of, row_block, parent_modes, parent_eigs
):
    subs = lax.axis_size("sub")
    parents = subs * parent_modes.shape[0]
    records, grams = records_and_grams(
        coupling, coupling_pairs, modes, mode_weights, parent_of, row_block, parents
    )
    scale = 1.0 / (coupling.shape[0] * modes.shape[2] * lax.axis_size("mode"))
    return strengths(
        parent_of, row_block, grams, records, parent_modes[0], parent_eigs, subs, scale
    )


def solution(mesh):
    in_specs = (
        P("sub", None, None),
        P("sub", None),
        P("sub", None, "mode"),
        P("sub", "mode"),
        P("sub", None),
        P("sub"),
        P("sub", None, None),
        P("sub", None),
    )
    return jax.shard_map(
        per_device, mesh=mesh, in_specs=in_specs, out_specs=P("sub", "mode"), check_vma=False
    )
```

```python
import functools

import jax
import jax.numpy as jnp
from jax import lax
from jax.experimental import pallas as pl
from jax.experimental.pallas import tpu as pltpu
from jax.sharding import PartitionSpec as P

MESH = pl.DeviceIdType.MESH
F32 = jnp.float32
BF16 = jnp.bfloat16
HALVES = 2


def dot(a, b, dims=((1,), (0,)), precision=None):
    return lax.dot_general(a, b, (dims, ((), ())), preferred_element_type=F32, precision=precision)


def exact(a, b, dims=((1,), (0,))):
    return dot(a, b, dims, lax.Precision.HIGHEST)


def split(x, terms):
    parts = []
    for _ in range(terms):
        part = x.astype(BF16)
        parts.append(part)
        x = x - part.astype(F32)
    return parts


def placed(record, right):
    zero = jnp.zeros_like(record)
    return jnp.concatenate(
        [jnp.where(right == 0, record, zero), jnp.where(right == 0, zero, record)], axis=0
    )


def record_kernel(
    children, group, parents, pair_ref, owner_ref, row_ref, coupling_ref, modes_ref, weight_ref, record_ref, gram_ref
):
    step = pl.program_id(0)

    @pl.when(step == 0)
    def _():
        @pl.loop(0, gram_ref.shape[0])
        def _(i):
            gram_ref[i] = jnp.zeros(gram_ref.shape[1:], F32)

    for i in range(group):
        child = step * group + i
        picked = jnp.concatenate(
            [modes_ref[i, pair_ref[child, k]] for k in range(pair_ref.shape[1])], axis=0
        )
        record = dot(coupling_ref[i], picked) * weight_ref[pl.ds(i, 1), :].astype(F32)
        record = record.astype(BF16)
        record_ref[i] = record
        block = row_ref[child]
        slot = ((block // 4) * 2 + (block // 2) % 2) * parents + owner_ref[child, 0]
        gram_ref[slot] += dot(record, placed(record, block % 2), ((1,), (1,)))


def records_and_grams(coupling, pairs, modes, weights, owner, row_block, parents):
    children, block, width = coupling.shape
    columns = modes.shape[2]
    blocks = modes.shape[1] // block
    group = 8
    return pl.pallas_call(
        functools.partial(record_kernel, children, group, parents),
        grid_spec=pltpu.PrefetchScalarGridSpec(
            num_scalar_prefetch=3,
            grid=(children // group,),
            in_specs=[
                pl.BlockSpec((group, block, width), lambda i, *_: (i, 0, 0)),
                pl.BlockSpec((group, blocks, block, columns), lambda i, *_: (i, 0, 0, 0)),
                pl.BlockSpec((group, columns), lambda i, *_: (i, 0)),
            ],
            out_specs=[
                pl.BlockSpec((group, block, columns), lambda i, *_: (i, 0, 0)),
                pl.BlockSpec((4 * parents, block, 2 * block), lambda i, *_: (0, 0, 0)),
            ],
        ),
        out_shape=[
            jax.ShapeDtypeStruct((children, block, columns), BF16),
            jax.ShapeDtypeStruct((4 * parents, block, 2 * block), F32),
        ],
        name="records",
    )(pairs, owner, row_block, coupling, modes.reshape(children, blocks, block, columns), weights)


def invert_block(matrix):
    size = matrix.shape[0]
    rows = 8
    lane = lax.broadcasted_iota(jnp.int32, (rows, size), 1)
    row = lax.broadcasted_iota(jnp.int32, (rows, size), 0)

    def turn(_, tiles):
        tiles = list(tiles)
        for j in range(0, rows, 2):
            first, second = lane == j, lane == j + 1
            pair = jnp.logical_or(first, second)

            def spread_row(i):
                return jnp.broadcast_to(tiles[0][i : i + 1, :], (rows, size))

            def spread_at(i, k):
                return jnp.broadcast_to(tiles[0][i : i + 1, k : k + 1], (rows, size))

            p, q = spread_row(j), spread_row(j + 1)
            a, b, c, d = (
                spread_at(j, j), spread_at(j, j + 1), spread_at(j + 1, j), spread_at(j + 1, j + 1)
            )
            scale = 1.0 / (a * d - b * c)
            a, b, c, d = a * scale, b * scale, c * scale, d * scale
            u = jnp.where(first, d, jnp.where(second, -b, d * p - b * q))
            v = jnp.where(first, -c, jnp.where(second, a, a * q - c * p))
            for t in range(len(tiles)):
                left = jnp.broadcast_to(tiles[t][:, j : j + 1], (rows, size))
                right = jnp.broadcast_to(tiles[t][:, j + 1 : j + 2], (rows, size))
                tiles[t] = jnp.where(pair, 0.0, tiles[t]) - left * u - right * v
            tiles[0] = jnp.where(row == j, u, jnp.where(row == j + 1, v, tiles[0]))
        tiles = tiles[1:] + tiles[:1]
        return tuple(pltpu.roll(t, size - rows, 1) for t in tiles)

    tiles = tuple(matrix[i * rows : (i + 1) * rows, :] for i in range(size // rows))
    tiles = lax.fori_loop(0, size // rows, turn, tiles)
    return jnp.concatenate(tiles, axis=0)


def exchange_kernel(
    subs, scale, owner_ref, row_ref, gram_ref, record_ref, parent_ref, eig_ref,
    out_ref,
    factor_ref, work,
    sib, recv_a, recv_b, recv_c, tile, tile_sib, spread, send_sem, recv_sem,
):
    zs = subs // 4
    me = lax.axis_index("sub")
    core = lax.axis_index("mode")
    z, y, x = me // 4, (me // 2) % 2, me % 2

    def place(zz, yy, xx):
        return ((zz * 2 + yy) * 2 + xx, core)

    sibling = (me, 1 - core)
    near_x, near_y = place(z, y, 1 - x), place(z, 1 - y, x)
    far = [place((z + d) % zs, y, x) for d in range(1, zs)]

    barrier = pltpu.get_barrier_semaphore()
    for peer in [sibling, near_x, near_y] + far:
        pl.semaphore_signal(barrier, inc=1, device_id=peer, device_id_type=MESH)
    pl.semaphore_wait(barrier, 3 + len(far))

    count = [0]

    def send(src, dst, peer):
        k = count[0]
        count[0] += 1
        copy = pltpu.make_async_remote_copy(
            src_ref=src, dst_ref=dst, send_sem=send_sem.at[k], recv_sem=recv_sem.at[k],
            device_id=peer, device_id_type=MESH,
        )
        copy.start()
        return copy

    copies = [send(gram_ref.at[1 - core, k], sib.at[k], sibling) for k in range(HALVES)]
    first = []
    for k in range(HALVES):
        copies[k].wait()

        @pl.loop(0, zs)
        def _(zz, k=k):
            for yy in range(2):
                for xx in range(2):
                    sib[k, zz, yy, xx] += gram_ref[core, k, zz, yy, xx]

        if k == 0:
            first.append(send(sib.at[0, :, :, 1 - x], recv_a.at[0], near_x))
        else:
            first.append(send(sib.at[1, :, 1 - y], recv_a.at[1], near_y))
    second = []
    for k in range(HALVES):
        first[k].wait()

        @pl.loop(0, zs)
        def _(zz, k=k):
            for i in range(2):
                mine = sib[0, zz, i, x] if k == 0 else sib[1, zz, y, i]
                recv_a[k, zz, i] += mine

        if k == 0:
            second.append(send(recv_a.at[0, :, 1 - y], recv_b.at[0], near_y))
        else:
            second.append(send(recv_a.at[1, :, 1 - x], recv_b.at[1], near_x))
    for k in range(HALVES):
        second[k].wait()

        @pl.loop(0, zs)
        def _(zz, k=k):
            recv_b[k, zz] += recv_a[k, zz, y if k == 0 else x]

    third = []
    for d in range(1, zs):
        there = (z + d) % zs
        third.append(send(recv_b.at[:, there], recv_c.at[d - 1], far[d - 1]))
    total = recv_b[:, z]
    for d in range(1, zs):
        third[d - 1].wait()
        total = total + recv_c[d - 1]
    tile[core] = total
    pair = send(tile.at[core], tile.at[core], sibling)
    pair.wait()

    size = parent_ref.shape[1]
    block = tile.shape[2]
    for h in range(2):
        for k in range(HALVES):
            both = split(tile[h, k], 3)
            for r in range(2):
                b = (h * 2 + k) * 2 + r
                rows = parent_ref[b * block : (b + 1) * block, :]
                part = sum(dot(t[:, r * block : (r + 1) * block], rows) for t in both)
                factor_ref[b * block : (b + 1) * block, :] = part
    total = jnp.zeros((size, size), F32)
    for part in split(factor_ref[...], 3):
        total = total + dot(parent_ref[...], part, ((0,), (0,)))
    diagonal = lax.broadcasted_iota(jnp.int32, (size, size), 0) == lax.broadcasted_iota(
        jnp.int32, (size, size), 1
    )
    work[...] = jnp.where(diagonal, eig_ref[...], 0.0) + total * scale

    half = size // 2
    top = invert_block(work[:half, :half])
    cross = work[:half, half:]
    ratio = exact(top, cross)
    corner = invert_block(work[half:, half:] - exact(cross, ratio, ((0,), (0,))))
    side = exact(ratio, corner)
    work[half:, half:] = corner
    work[:half, half:] = -side
    work[half:, :half] = -side.T
    work[:half, :half] = top + exact(side, ratio, ((1,), (1,)))

    span = 2 * HALVES * block
    mine = parent_ref[pl.ds(pl.multiple_of(core * span, span), span), :]
    turned = sum(dot(mine, part) for part in split(work[...], 3))
    factor_ref[:span, :] = turned
    for k in range(HALVES):
        for r in range(2):
            at = (k * 2 + r) * block
            rows = factor_ref[at : at + block, :]
            base = parent_ref[pl.ds(pl.multiple_of(core * span + at, block), block), :]
            value = sum(dot(part, base, ((1,), (1,))) for part in split(rows, 2))
            tile_sib[k, :, r * block : (r + 1) * block] = value.astype(BF16)

    for k in range(HALVES):
        spread[core, k, z, y, x] = tile_sib[k]
    own = [send(spread.at[core, :, z, y, x], spread.at[core, :, z, y, x], peer) for peer in far]
    for copy in own:
        copy.wait()
    a = spread.at[core, 0, :, y, x]
    b = spread.at[core, 1, :, y, x]
    up = [send(a, a, near_y), send(b, b, near_x)]
    for copy in up:
        copy.wait()
    a = spread.at[core, 0, :, :, x]
    b = spread.at[core, 1, :, y]
    last = [send(a, a, near_x), send(b, b, near_y)]
    across = [
        send(spread.at[core, 0, :, :, x], spread.at[core, 0, :, :, x], sibling),
        send(spread.at[core, 1, :, y], spread.at[core, 1, :, y], sibling),
    ]
    for copy in last:
        copy.wait()
    across.append(send(spread.at[core, 0, :, :, 1 - x], spread.at[core, 0, :, :, 1 - x], sibling))
    across.append(send(spread.at[core, 1, :, 1 - y], spread.at[core, 1, :, 1 - y], sibling))
    for copy in across:
        copy.wait()

    group = 8

    @pl.loop(0, record_ref.shape[0] // group)
    def _(step):
        values = []
        for i in range(group):
            child = step * group + i
            record = record_ref[child]
            parent, row = owner_ref[child, 0], row_ref[child]
            form = spread[row // 4, (row // 2) % 2, parent // 4, (parent // 2) % 2, parent % 2]
            pushed = dot(form, placed(record, row % 2))
            values.append(jnp.sum(record.astype(F32) * pushed, axis=0, keepdims=True))
        out_ref[pl.ds(pl.multiple_of(step * group, group), group), :] = (
            jnp.concatenate(values, axis=0) / size
        )


def strengths(owner, row_block, grams, records, parent, eigs, subs, scale):
    children, block, columns = records.shape
    rows, size = parent.shape
    zs = subs // 4
    tile = (block, 2 * block)
    copies = 16 + 2 * (zs - 1)
    vmem = pl.BlockSpec(memory_space=pltpu.VMEM)
    smem = pl.BlockSpec(memory_space=pltpu.SMEM)
    return pl.pallas_call(
        functools.partial(exchange_kernel, subs, scale),
        in_specs=[smem, smem, vmem, vmem, vmem, vmem],
        out_specs=vmem,
        out_shape=jax.ShapeDtypeStruct((children, columns), F32),
        scratch_shapes=[
            pltpu.VMEM((rows, size), F32),
            pltpu.VMEM((size, size), F32),
            pltpu.VMEM((HALVES, zs, 2, 2) + tile, F32),
            pltpu.VMEM((HALVES, zs, 2) + tile, F32),
            pltpu.VMEM((HALVES, zs) + tile, F32),
            pltpu.VMEM((max(1, zs - 1), HALVES) + tile, F32),
            pltpu.VMEM((2, HALVES) + tile, F32),
            pltpu.VMEM((HALVES,) + tile, BF16),
            pltpu.VMEM((2, HALVES, zs, 2, 2) + tile, BF16),
            pltpu.SemaphoreType.DMA((copies,)),
            pltpu.SemaphoreType.DMA((copies,)),
        ],
        compiler_params=pltpu.CompilerParams(
            collective_id=0, has_side_effects=True, vmem_limit_bytes=60 << 20
        ),
        name="exchange",
    )(owner, row_block, grams.reshape((2, HALVES, zs, 2, 2) + tile), records, parent, eigs)


def per_device(
    coupling, coupling_pairs, modes, mode_weights, parent_of, row_block, parent_modes, parent_eigs
):
    subs = lax.axis_size("sub")
    parents = subs * parent_modes.shape[0]
    records, grams = records_and_grams(
        coupling, coupling_pairs, modes, mode_weights, parent_of, row_block, parents
    )
    scale = 1.0 / (coupling.shape[0] * modes.shape[2] * lax.axis_size("mode"))
    return strengths(
        parent_of, row_block, grams, records, parent_modes[0], parent_eigs, subs, scale
    )


def solution(mesh):
    in_specs = (
        P("sub", None, None),
        P("sub", None),
        P("sub", None, "mode"),
        P("sub", "mode"),
        P("sub", None),
        P("sub"),
        P("sub", None, None),
        P("sub", None),
    )
    return jax.shard_map(
        per_device, mesh=mesh, in_specs=in_specs, out_specs=P("sub", "mode"), check_vma=False
    )
```

```python
import functools

import jax
import jax.numpy as jnp
from jax import lax
from jax.experimental import pallas as pl
from jax.experimental.pallas import tpu as pltpu
from jax.sharding import PartitionSpec as P

MESH = pl.DeviceIdType.MESH
F32 = jnp.float32
BF16 = jnp.bfloat16
HALVES = 2


def dot(a, b, dims=((1,), (0,)), precision=None):
    return lax.dot_general(a, b, (dims, ((), ())), preferred_element_type=F32, precision=precision)


def exact(a, b, dims=((1,), (0,))):
    return dot(a, b, dims, lax.Precision.HIGHEST)


def split(x, terms):
    parts = []
    for _ in range(terms):
        part = x.astype(BF16)
        parts.append(part)
        x = x - part.astype(F32)
    return parts


def placed(record, right):
    zero = jnp.zeros_like(record)
    return jnp.concatenate(
        [jnp.where(right == 0, record, zero), jnp.where(right == 0, zero, record)], axis=0
    )


def below(block):
    shape = (block, 2 * block)
    row = lax.broadcasted_iota(jnp.int32, shape, 0)
    lane = lax.broadcasted_iota(jnp.int32, shape, 1)
    return row, jnp.where(lane < block, lane, lane - block)


def record_kernel(
    group, parents, index_ref, coupling_ref, modes_ref, weight_ref, record_ref, pack_ref, gram_ref
):
    step = pl.program_id(0)

    @pl.when(step == 0)
    def _():
        @pl.loop(0, gram_ref.shape[0])
        def _(i):
            gram_ref[i] = jnp.zeros(gram_ref.shape[1:], F32)

    pairs = index_ref.shape[0] - 2
    products = []
    for i in range(group):
        child = step * group + i
        picked = jnp.concatenate(
            [modes_ref[i, index_ref[2 + k, child]] for k in range(pairs)], axis=0
        )
        record = dot(coupling_ref[i], picked) * weight_ref[pl.ds(i, 1), :].astype(F32)
        record = record.astype(BF16)
        record_ref[i] = record
        side = index_ref[1, child] % 2
        products.append(dot(record, placed(record, side), ((1,), (1,))))
    for i in range(group):
        child = step * group + i
        gram_ref[(index_ref[1, child] // 2) * parents + index_ref[0, child]] += products[i]

    @pl.when(step == pl.num_programs(0) - 1)
    def _():
        block = gram_ref.shape[1]
        part = block // 2
        row, column = below(block)

        @pl.loop(0, parents)
        def _(p):
            for h in range(2):
                high, low = h * 2 * parents + p, (h * 2 + 1) * parents + p
                upper, lower = gram_ref[high], gram_ref[low]
                packed = jnp.where(row <= column, upper, lower)
                diagonal = jnp.sum(jnp.where(row == column, lower, 0.0), axis=0, keepdims=True)
                pack_ref[high, :part] = packed[:part]
                pack_ref[high, part:] = jnp.broadcast_to(diagonal, (8, 2 * block))
                pack_ref[low, :part] = packed[part:]
                pack_ref[low, part:] = jnp.zeros((8, 2 * block), F32)


def records_and_grams(index, coupling, modes, weights, parents):
    children, block, width = coupling.shape
    columns = modes.shape[2]
    blocks = modes.shape[1] // block
    group = 16
    packed = (4 * parents, block // 2 + 8, 2 * block)
    return pl.pallas_call(
        functools.partial(record_kernel, group, parents),
        grid_spec=pltpu.PrefetchScalarGridSpec(
            num_scalar_prefetch=1,
            grid=(children // group,),
            in_specs=[
                pl.BlockSpec((group, block, width), lambda i, *_: (i, 0, 0)),
                pl.BlockSpec((group, blocks, block, columns), lambda i, *_: (i, 0, 0, 0)),
                pl.BlockSpec((group, columns), lambda i, *_: (i, 0)),
            ],
            out_specs=[
                pl.BlockSpec((group, block, columns), lambda i, *_: (i, 0, 0)),
                pl.BlockSpec(packed, lambda i, *_: (0, 0, 0)),
            ],
            scratch_shapes=[pltpu.VMEM((4 * parents, block, 2 * block), F32)],
        ),
        out_shape=[
            jax.ShapeDtypeStruct((children, block, columns), BF16),
            jax.ShapeDtypeStruct(packed, F32),
        ],
        name="records",
    )(index, coupling, modes.reshape(children, blocks, block, columns), weights)


def invert_block(matrix):
    size = matrix.shape[0]
    rows = 8
    lane = lax.broadcasted_iota(jnp.int32, (rows, size), 1)
    row = lax.broadcasted_iota(jnp.int32, (rows, size), 0)

    def turn(_, tiles):
        tiles = list(tiles)
        for j in range(0, rows, 2):
            first, second = lane == j, lane == j + 1
            pair = jnp.logical_or(first, second)

            def spread_row(i):
                return jnp.broadcast_to(tiles[0][i : i + 1, :], (rows, size))

            def spread_at(i, k):
                return jnp.broadcast_to(tiles[0][i : i + 1, k : k + 1], (rows, size))

            p, q = spread_row(j), spread_row(j + 1)
            a, b, c, d = (
                spread_at(j, j), spread_at(j, j + 1), spread_at(j + 1, j), spread_at(j + 1, j + 1)
            )
            scale = 1.0 / (a * d - b * c)
            a, b, c, d = a * scale, b * scale, c * scale, d * scale
            u = jnp.where(first, d, jnp.where(second, -b, d * p - b * q))
            v = jnp.where(first, -c, jnp.where(second, a, a * q - c * p))
            for t in range(len(tiles)):
                left = jnp.broadcast_to(tiles[t][:, j : j + 1], (rows, size))
                right = jnp.broadcast_to(tiles[t][:, j + 1 : j + 2], (rows, size))
                tiles[t] = jnp.where(pair, 0.0, tiles[t]) - left * u - right * v
            tiles[0] = jnp.where(row == j, u, jnp.where(row == j + 1, v, tiles[0]))
        tiles = tiles[1:] + tiles[:1]
        return tuple(pltpu.roll(t, size - rows, 1) for t in tiles)

    tiles = tuple(matrix[i * rows : (i + 1) * rows, :] for i in range(size // rows))
    tiles = lax.fori_loop(0, size // rows, turn, tiles)
    return jnp.concatenate(tiles, axis=0)


def exchange_kernel(
    subs, scale, index_ref, gram_ref, record_ref, parent_ref, eig_ref,
    out_ref,
    factor_ref, work,
    sib, recv_a, recv_b, recv_c, tile, tile_sib, spread, send_sem, recv_sem,
):
    zs = subs // 4
    me = lax.axis_index("sub")
    core = lax.axis_index("mode")
    z, y, x = me // 4, (me // 2) % 2, me % 2

    def place(zz, yy, xx):
        return ((zz * 2 + yy) * 2 + xx, core)

    sibling = (me, 1 - core)
    near_x, near_y = place(z, y, 1 - x), place(z, 1 - y, x)
    far = [place((z + d) % zs, y, x) for d in range(1, zs)]

    barrier = pltpu.get_barrier_semaphore()
    for peer in [sibling, near_x, near_y] + far:
        pl.semaphore_signal(barrier, inc=1, device_id=peer, device_id_type=MESH)
    pl.semaphore_wait(barrier, 3 + len(far))

    count = [0]

    def send(src, dst, peer):
        k = count[0]
        count[0] += 1
        copy = pltpu.make_async_remote_copy(
            src_ref=src, dst_ref=dst, send_sem=send_sem.at[k], recv_sem=recv_sem.at[k],
            device_id=peer, device_id_type=MESH,
        )
        copy.start()
        return copy

    copies = [send(gram_ref.at[1 - core, k], sib.at[k], sibling) for k in range(HALVES)]
    first = []
    for k in range(HALVES):
        copies[k].wait()

        @pl.loop(0, zs)
        def _(zz, k=k):
            for yy in range(2):
                for xx in range(2):
                    sib[k, zz, yy, xx] += gram_ref[core, k, zz, yy, xx]

        if k == 0:
            first.append(send(sib.at[0, :, :, 1 - x], recv_a.at[0], near_x))
        else:
            first.append(send(sib.at[1, :, 1 - y], recv_a.at[1], near_y))
    second = []
    for k in range(HALVES):
        first[k].wait()

        @pl.loop(0, zs)
        def _(zz, k=k):
            for i in range(2):
                mine = sib[0, zz, i, x] if k == 0 else sib[1, zz, y, i]
                recv_a[k, zz, i] += mine

        if k == 0:
            second.append(send(recv_a.at[0, :, 1 - y], recv_b.at[0], near_y))
        else:
            second.append(send(recv_a.at[1, :, 1 - x], recv_b.at[1], near_x))
    for k in range(HALVES):
        second[k].wait()

        @pl.loop(0, zs)
        def _(zz, k=k):
            recv_b[k, zz] += recv_a[k, zz, y if k == 0 else x]

    third = []
    for d in range(1, zs):
        there = (z + d) % zs
        third.append(send(recv_b.at[:, there], recv_c.at[d - 1], far[d - 1]))
    total = recv_b[:, z]
    for d in range(1, zs):
        third[d - 1].wait()
        total = total + recv_c[d - 1]
    tile[core] = total
    pair = send(tile.at[core], tile.at[core], sibling)
    pair.wait()

    size = parent_ref.shape[1]
    block = spread.shape[-2]
    part = block // 2
    row, column = below(block)
    for h in range(2):
        packed = jnp.concatenate([tile[h, 0, :part], tile[h, 1, :part]], axis=0)
        lower_diagonal = jnp.broadcast_to(tile[h, 0, part : part + 1], packed.shape)
        for k in range(HALVES):
            inside = row < column if k == 0 else row > column
            middle = packed if k == 0 else lower_diagonal
            triangle = jnp.where(inside, packed, jnp.where(row == column, 0.5 * middle, 0.0))
            terms = split(triangle, 3)
            for r in range(2):
                b = (h * 2 + k) * 2 + r
                rows = parent_ref[b * block : (b + 1) * block, :]
                factor_ref[b * block : (b + 1) * block, :] = sum(
                    dot(t[:, r * block : (r + 1) * block], rows) for t in terms
                )
    total = jnp.zeros((size, size), F32)
    for term in split(factor_ref[...], 3):
        total = total + dot(parent_ref[...], term, ((0,), (0,)))
    diagonal = lax.broadcasted_iota(jnp.int32, (size, size), 0) == lax.broadcasted_iota(
        jnp.int32, (size, size), 1
    )
    work[...] = jnp.where(diagonal, eig_ref[...], 0.0) + (total + total.T) * scale

    half = size // 2
    top = invert_block(work[:half, :half])
    cross = work[:half, half:]
    ratio = exact(top, cross)
    corner = invert_block(work[half:, half:] - exact(cross, ratio, ((0,), (0,))))
    side = exact(ratio, corner)
    work[half:, half:] = corner
    work[:half, half:] = -side
    work[half:, :half] = -side.T
    work[:half, :half] = top + exact(side, ratio, ((1,), (1,)))

    span = 2 * HALVES * block
    mine = parent_ref[pl.ds(pl.multiple_of(core * span, span), span), :]
    turned = sum(dot(mine, part) for part in split(work[...], 3))
    factor_ref[:span, :] = turned
    for k in range(HALVES):
        for r in range(2):
            at = (k * 2 + r) * block
            rows = factor_ref[at : at + block, :]
            base = parent_ref[pl.ds(pl.multiple_of(core * span + at, block), block), :]
            value = sum(dot(part, base, ((1,), (1,))) for part in split(rows, 2))
            tile_sib[k, :, r * block : (r + 1) * block] = value.astype(BF16)

    for k in range(HALVES):
        spread[core, k, z, y, x] = tile_sib[k]
    own = [send(spread.at[core, :, z, y, x], spread.at[core, :, z, y, x], peer) for peer in far]
    for copy in own:
        copy.wait()
    a = spread.at[core, 0, :, y, x]
    b = spread.at[core, 1, :, y, x]
    up = [send(a, a, near_y), send(b, b, near_x)]
    for copy in up:
        copy.wait()
    a = spread.at[core, 0, :, :, x]
    b = spread.at[core, 1, :, y]
    last = [send(a, a, near_x), send(b, b, near_y)]
    across = [
        send(spread.at[core, 0, :, :, x], spread.at[core, 0, :, :, x], sibling),
        send(spread.at[core, 1, :, y], spread.at[core, 1, :, y], sibling),
    ]
    for copy in last:
        copy.wait()
    across.append(send(spread.at[core, 0, :, :, 1 - x], spread.at[core, 0, :, :, 1 - x], sibling))
    across.append(send(spread.at[core, 1, :, 1 - y], spread.at[core, 1, :, 1 - y], sibling))
    for copy in across:
        copy.wait()

    group = 8

    @pl.loop(0, record_ref.shape[0] // group)
    def _(step):
        values = []
        for i in range(group):
            child = step * group + i
            record = record_ref[child]
            parent, place_row = index_ref[0, child], index_ref[1, child]
            form = spread[place_row // 4, (place_row // 2) % 2, parent // 4, (parent // 2) % 2, parent % 2]
            pushed = dot(form, placed(record, place_row % 2))
            values.append(jnp.sum(record.astype(F32) * pushed, axis=0, keepdims=True))
        out_ref[pl.ds(pl.multiple_of(step * group, group), group), :] = (
            jnp.concatenate(values, axis=0) / size
        )


def strengths(index, grams, records, parent, eigs, subs, scale):
    children, block, columns = records.shape
    rows, size = parent.shape
    zs = subs // 4
    tile = (block, 2 * block)
    packed = grams.shape[1:]
    copies = 16 + 2 * (zs - 1)
    vmem = pl.BlockSpec(memory_space=pltpu.VMEM)
    smem = pl.BlockSpec(memory_space=pltpu.SMEM)
    return pl.pallas_call(
        functools.partial(exchange_kernel, subs, scale),
        in_specs=[smem, vmem, vmem, vmem, vmem],
        out_specs=vmem,
        out_shape=jax.ShapeDtypeStruct((children, columns), F32),
        scratch_shapes=[
            pltpu.VMEM((rows, size), F32),
            pltpu.VMEM((size, size), F32),
            pltpu.VMEM((HALVES, zs, 2, 2) + packed, F32),
            pltpu.VMEM((HALVES, zs, 2) + packed, F32),
            pltpu.VMEM((HALVES, zs) + packed, F32),
            pltpu.VMEM((max(1, zs - 1), HALVES) + packed, F32),
            pltpu.VMEM((2, HALVES) + packed, F32),
            pltpu.VMEM((HALVES,) + tile, BF16),
            pltpu.VMEM((2, HALVES, zs, 2, 2) + tile, BF16),
            pltpu.SemaphoreType.DMA((copies,)),
            pltpu.SemaphoreType.DMA((copies,)),
        ],
        compiler_params=pltpu.CompilerParams(
            collective_id=0, has_side_effects=True, vmem_limit_bytes=60 << 20
        ),
        name="exchange",
    )(index, grams.reshape((2, HALVES, zs, 2, 2) + packed), records, parent, eigs)


def per_device(
    coupling, coupling_pairs, modes, mode_weights, parent_of, row_block, parent_modes, parent_eigs
):
    subs = lax.axis_size("sub")
    parents = subs * parent_modes.shape[0]
    index = jnp.concatenate([parent_of.T, row_block[None], coupling_pairs.T], axis=0)
    records, grams = records_and_grams(index, coupling, modes, mode_weights, parents)
    scale = 1.0 / (coupling.shape[0] * modes.shape[2] * lax.axis_size("mode"))
    return strengths(
        index, grams, records, parent_modes[0], parent_eigs, subs, scale
    )


def solution(mesh):
    in_specs = (
        P("sub", None, None),
        P("sub", None),
        P("sub", None, "mode"),
        P("sub", "mode"),
        P("sub", None),
        P("sub"),
        P("sub", None, None),
        P("sub", None),
    )
    return jax.shard_map(
        per_device, mesh=mesh, in_specs=in_specs, out_specs=P("sub", "mode"), check_vma=False
    )
```

```python
import functools

import jax
import jax.numpy as jnp
from jax import lax
from jax.experimental import pallas as pl
from jax.experimental.pallas import tpu as pltpu
from jax.sharding import PartitionSpec as P

MESH = pl.DeviceIdType.MESH
F32 = jnp.float32
BF16 = jnp.bfloat16
HALVES = 2


def dot(a, b, dims=((1,), (0,)), precision=None):
    return lax.dot_general(a, b, (dims, ((), ())), preferred_element_type=F32, precision=precision)


def exact(a, b, dims=((1,), (0,))):
    return dot(a, b, dims, lax.Precision.HIGHEST)


def split(x, terms):
    parts = []
    for _ in range(terms):
        part = x.astype(BF16)
        parts.append(part)
        x = x - part.astype(F32)
    return parts


def placed(record, right):
    zero = jnp.zeros_like(record)
    return jnp.concatenate(
        [jnp.where(right == 0, record, zero), jnp.where(right == 0, zero, record)], axis=0
    )


def below(block):
    shape = (block, 2 * block)
    row = lax.broadcasted_iota(jnp.int32, shape, 0)
    lane = lax.broadcasted_iota(jnp.int32, shape, 1)
    return row, jnp.where(lane < block, lane, lane - block)


def record_kernel(
    group, parents, index_ref, coupling_ref, modes_ref, weight_ref, record_ref, pack_ref, gram_ref
):
    step = pl.program_id(0)

    @pl.when(step == 0)
    def _():
        @pl.loop(0, gram_ref.shape[0])
        def _(i):
            gram_ref[i] = jnp.zeros(gram_ref.shape[1:], F32)

    pairs = index_ref.shape[0] - 2
    products = []
    for i in range(group):
        child = step * group + i
        picked = jnp.concatenate(
            [modes_ref[i, index_ref[2 + k, child]] for k in range(pairs)], axis=0
        )
        record = dot(coupling_ref[i], picked) * weight_ref[pl.ds(i, 1), :].astype(F32)
        record = record.astype(BF16)
        record_ref[i] = record
        side = index_ref[1, child] % 2
        products.append(dot(record, placed(record, side), ((1,), (1,))))
    for i in range(group):
        child = step * group + i
        gram_ref[(index_ref[1, child] // 2) * parents + index_ref[0, child]] += products[i]

    @pl.when(step == pl.num_programs(0) - 1)
    def _():
        block = gram_ref.shape[1]
        part = block // 2
        row, column = below(block)

        @pl.loop(0, parents)
        def _(p):
            for h in range(2):
                high, low = h * 2 * parents + p, (h * 2 + 1) * parents + p
                upper, lower = gram_ref[high], gram_ref[low]
                packed = jnp.where(row <= column, upper, lower)
                diagonal = jnp.sum(jnp.where(row == column, lower, 0.0), axis=0, keepdims=True)
                pack_ref[high, :part] = packed[:part]
                pack_ref[high, part:] = jnp.broadcast_to(diagonal, (8, 2 * block))
                pack_ref[low, :part] = packed[part:]
                pack_ref[low, part:] = jnp.zeros((8, 2 * block), F32)


def records_and_grams(index, coupling, modes, weights, parents):
    children, block, width = coupling.shape
    columns = modes.shape[2]
    blocks = modes.shape[1] // block
    group = 16
    packed = (4 * parents, block // 2 + 8, 2 * block)
    return pl.pallas_call(
        functools.partial(record_kernel, group, parents),
        grid_spec=pltpu.PrefetchScalarGridSpec(
            num_scalar_prefetch=1,
            grid=(children // group,),
            in_specs=[
                pl.BlockSpec((group, block, width), lambda i, *_: (i, 0, 0)),
                pl.BlockSpec((group, blocks, block, columns), lambda i, *_: (i, 0, 0, 0)),
                pl.BlockSpec((group, columns), lambda i, *_: (i, 0)),
            ],
            out_specs=[
                pl.BlockSpec((group, block, columns), lambda i, *_: (i, 0, 0)),
                pl.BlockSpec(packed, lambda i, *_: (0, 0, 0)),
            ],
            scratch_shapes=[pltpu.VMEM((4 * parents, block, 2 * block), F32)],
        ),
        out_shape=[
            jax.ShapeDtypeStruct((children, block, columns), BF16),
            jax.ShapeDtypeStruct(packed, F32),
        ],
        name="records",
    )(index, coupling, modes.reshape(children, blocks, block, columns), weights)


def invert_block(matrix):
    size = matrix.shape[0]
    rows = 8
    lane = lax.broadcasted_iota(jnp.int32, (rows, size), 1)
    row = lax.broadcasted_iota(jnp.int32, (rows, size), 0)

    def turn(_, tiles):
        tiles = list(tiles)
        for j in range(0, rows, 2):
            first, second = lane == j, lane == j + 1
            pair = jnp.logical_or(first, second)

            def spread_row(i):
                return jnp.broadcast_to(tiles[0][i : i + 1, :], (rows, size))

            def spread_at(i, k):
                return jnp.broadcast_to(tiles[0][i : i + 1, k : k + 1], (rows, size))

            p, q = spread_row(j), spread_row(j + 1)
            a, b, c, d = (
                spread_at(j, j), spread_at(j, j + 1), spread_at(j + 1, j), spread_at(j + 1, j + 1)
            )
            scale = 1.0 / (a * d - b * c)
            a, b, c, d = a * scale, b * scale, c * scale, d * scale
            u = jnp.where(first, d, jnp.where(second, -b, d * p - b * q))
            v = jnp.where(first, -c, jnp.where(second, a, a * q - c * p))
            for t in range(len(tiles)):
                left = jnp.broadcast_to(tiles[t][:, j : j + 1], (rows, size))
                right = jnp.broadcast_to(tiles[t][:, j + 1 : j + 2], (rows, size))
                tiles[t] = jnp.where(pair, 0.0, tiles[t]) - left * u - right * v
            tiles[0] = jnp.where(row == j, u, jnp.where(row == j + 1, v, tiles[0]))
        tiles = tiles[1:] + tiles[:1]
        return tuple(pltpu.roll(t, size - rows, 1) for t in tiles)

    tiles = tuple(matrix[i * rows : (i + 1) * rows, :] for i in range(size // rows))
    tiles = lax.fori_loop(0, size // rows, turn, tiles)
    return jnp.concatenate(tiles, axis=0)


def exchange_kernel(
    subs, scale, index_ref, gram_ref, record_ref, parent_ref, eig_ref,
    out_ref,
    factor_ref, work,
    sib, recv_a, recv_b, recv_c, tile, tile_sib, spread, send_sem, recv_sem,
):
    zs = subs // 4
    me = lax.axis_index("sub")
    core = lax.axis_index("mode")
    z, y, x = me // 4, (me // 2) % 2, me % 2

    def place(zz, yy, xx):
        return ((zz * 2 + yy) * 2 + xx, core)

    sibling = (me, 1 - core)
    near_x, near_y = place(z, y, 1 - x), place(z, 1 - y, x)
    far = [place((z + d) % zs, y, x) for d in range(1, zs)]

    barrier = pltpu.get_barrier_semaphore()
    for peer in [sibling, near_x, near_y] + far:
        pl.semaphore_signal(barrier, inc=1, device_id=peer, device_id_type=MESH)
    pl.semaphore_wait(barrier, 3 + len(far))

    count = [0]

    def send(src, dst, peer):
        k = count[0]
        count[0] += 1
        copy = pltpu.make_async_remote_copy(
            src_ref=src, dst_ref=dst, send_sem=send_sem.at[k], recv_sem=recv_sem.at[k],
            device_id=peer, device_id_type=MESH,
        )
        copy.start()
        return copy

    copies = [send(gram_ref.at[1 - core, k], sib.at[k], sibling) for k in range(HALVES)]
    first = []
    for k in range(HALVES):
        copies[k].wait()

        @pl.loop(0, zs)
        def _(zz, k=k):
            for yy in range(2):
                for xx in range(2):
                    sib[k, zz, yy, xx] += gram_ref[core, k, zz, yy, xx]

        if k == 0:
            first.append(send(sib.at[0, :, :, 1 - x], recv_a.at[0], near_x))
        else:
            first.append(send(sib.at[1, :, 1 - y], recv_a.at[1], near_y))
    second = []
    for k in range(HALVES):
        first[k].wait()

        @pl.loop(0, zs)
        def _(zz, k=k):
            for i in range(2):
                mine = sib[0, zz, i, x] if k == 0 else sib[1, zz, y, i]
                recv_a[k, zz, i] += mine

        if k == 0:
            second.append(send(recv_a.at[0, :, 1 - y], recv_b.at[0], near_y))
        else:
            second.append(send(recv_a.at[1, :, 1 - x], recv_b.at[1], near_x))
    for k in range(HALVES):
        second[k].wait()

        @pl.loop(0, zs)
        def _(zz, k=k):
            recv_b[k, zz] += recv_a[k, zz, y if k == 0 else x]

    third = []
    for d in range(1, zs):
        there = (z + d) % zs
        third.append(send(recv_b.at[:, there], recv_c.at[d - 1], far[d - 1]))
    total = recv_b[:, z]
    for d in range(1, zs):
        third[d - 1].wait()
        total = total + recv_c[d - 1]
    tile[core] = total
    pair = send(tile.at[core], tile.at[core], sibling)
    pair.wait()

    size = parent_ref.shape[1]
    block = spread.shape[-2]
    part = block // 2
    row, column = below(block)
    for h in range(2):
        packed = jnp.concatenate([tile[h, 0, :part], tile[h, 1, :part]], axis=0)
        lower_diagonal = jnp.broadcast_to(tile[h, 0, part : part + 1], packed.shape)
        for k in range(HALVES):
            inside = row < column if k == 0 else row > column
            middle = packed if k == 0 else lower_diagonal
            triangle = jnp.where(inside, packed, jnp.where(row == column, 0.5 * middle, 0.0))
            terms = split(triangle, 3)
            for r in range(2):
                b = (h * 2 + k) * 2 + r
                rows = parent_ref[b * block : (b + 1) * block, :]
                factor_ref[b * block : (b + 1) * block, :] = sum(
                    dot(t[:, r * block : (r + 1) * block], rows) for t in terms
                )
    total = jnp.zeros((size, size), F32)
    for term in split(factor_ref[...], 3):
        total = total + dot(parent_ref[...], term, ((0,), (0,)))
    diagonal = lax.broadcasted_iota(jnp.int32, (size, size), 0) == lax.broadcasted_iota(
        jnp.int32, (size, size), 1
    )
    work[...] = jnp.where(diagonal, eig_ref[...], 0.0) + (total + total.T) * scale

    half = size // 2
    top = invert_block(work[:half, :half])
    cross = work[:half, half:]
    ratio = exact(top, cross)
    corner = invert_block(work[half:, half:] - exact(cross, ratio, ((0,), (0,))))
    side = exact(ratio, corner)
    work[half:, half:] = corner
    work[:half, half:] = -side
    work[half:, :half] = -side.T
    work[:half, :half] = top + exact(side, ratio, ((1,), (1,)))

    span = 2 * HALVES * block
    mine = parent_ref[pl.ds(pl.multiple_of(core * span, span), span), :]
    turned = sum(dot(mine, part) for part in split(work[...], 3))
    factor_ref[:span, :] = turned
    for k in range(HALVES):
        for r in range(2):
            at = (k * 2 + r) * block
            rows = factor_ref[at : at + block, :]
            base = parent_ref[pl.ds(pl.multiple_of(core * span + at, block), block), :]
            value = sum(dot(part, base, ((1,), (1,))) for part in split(rows, 2))
            tile_sib[k, :, r * block : (r + 1) * block] = value.astype(BF16)

    for k in range(HALVES):
        spread[core, k, z, y, x] = tile_sib[k]
    own = [send(spread.at[core, :, z, y, x], spread.at[core, :, z, y, x], peer) for peer in far]
    for copy in own:
        copy.wait()
    a = spread.at[core, 0, :, y, x]
    b = spread.at[core, 1, :, y, x]
    up = [send(a, a, near_y), send(b, b, near_x)]
    across = [send(a, a, sibling), send(b, b, sibling)]
    a = spread.at[core, 0, :, :, x]
    b = spread.at[core, 1, :, y]
    last = []
    up[0].wait()
    last.append(send(a, a, near_x))
    up[1].wait()
    last.append(send(b, b, near_y))
    a = spread.at[core, 0, :, 1 - y, x]
    b = spread.at[core, 1, :, y, 1 - x]
    across += [send(a, a, sibling), send(b, b, sibling)]
    a = spread.at[core, 0, :, :, 1 - x]
    b = spread.at[core, 1, :, 1 - y]
    last[0].wait()
    across.append(send(a, a, sibling))
    last[1].wait()
    across.append(send(b, b, sibling))
    for copy in across:
        copy.wait()

    group = 8

    @pl.loop(0, record_ref.shape[0] // group)
    def _(step):
        values = []
        for i in range(group):
            child = step * group + i
            record = record_ref[child]
            parent, place_row = index_ref[0, child], index_ref[1, child]
            form = spread[place_row // 4, (place_row // 2) % 2, parent // 4, (parent // 2) % 2, parent % 2]
            pushed = dot(form, placed(record, place_row % 2))
            values.append(jnp.sum(record.astype(F32) * pushed, axis=0, keepdims=True))
        out_ref[pl.ds(pl.multiple_of(step * group, group), group), :] = (
            jnp.concatenate(values, axis=0) / size
        )


def strengths(index, grams, records, parent, eigs, subs, scale):
    children, block, columns = records.shape
    rows, size = parent.shape
    zs = subs // 4
    tile = (block, 2 * block)
    packed = grams.shape[1:]
    copies = 20 + 2 * (zs - 1)
    vmem = pl.BlockSpec(memory_space=pltpu.VMEM)
    smem = pl.BlockSpec(memory_space=pltpu.SMEM)
    return pl.pallas_call(
        functools.partial(exchange_kernel, subs, scale),
        in_specs=[smem, vmem, vmem, vmem, vmem],
        out_specs=vmem,
        out_shape=jax.ShapeDtypeStruct((children, columns), F32),
        scratch_shapes=[
            pltpu.VMEM((rows, size), F32),
            pltpu.VMEM((size, size), F32),
            pltpu.VMEM((HALVES, zs, 2, 2) + packed, F32),
            pltpu.VMEM((HALVES, zs, 2) + packed, F32),
            pltpu.VMEM((HALVES, zs) + packed, F32),
            pltpu.VMEM((max(1, zs - 1), HALVES) + packed, F32),
            pltpu.VMEM((2, HALVES) + packed, F32),
            pltpu.VMEM((HALVES,) + tile, BF16),
            pltpu.VMEM((2, HALVES, zs, 2, 2) + tile, BF16),
            pltpu.SemaphoreType.DMA((copies,)),
            pltpu.SemaphoreType.DMA((copies,)),
        ],
        compiler_params=pltpu.CompilerParams(
            collective_id=0, has_side_effects=True, vmem_limit_bytes=60 << 20
        ),
        name="exchange",
    )(index, grams.reshape((2, HALVES, zs, 2, 2) + packed), records, parent, eigs)


def per_device(
    coupling, coupling_pairs, modes, mode_weights, parent_of, row_block, parent_modes, parent_eigs
):
    subs = lax.axis_size("sub")
    parents = subs * parent_modes.shape[0]
    index = jnp.concatenate([parent_of.T, row_block[None], coupling_pairs.T], axis=0)
    records, grams = records_and_grams(index, coupling, modes, mode_weights, parents)
    scale = 1.0 / (coupling.shape[0] * modes.shape[2] * lax.axis_size("mode"))
    return strengths(
        index, grams, records, parent_modes[0], parent_eigs, subs, scale
    )


def solution(mesh):
    in_specs = (
        P("sub", None, None),
        P("sub", None),
        P("sub", None, "mode"),
        P("sub", "mode"),
        P("sub", None),
        P("sub"),
        P("sub", None, None),
        P("sub", None),
    )
    return jax.shard_map(
        per_device, mesh=mesh, in_specs=in_specs, out_specs=P("sub", "mode"), check_vma=False
    )
```
